512 devices in a mesh: dp: 8 (over x, core), tensor: 64 (over z, y).
Axes of the slice: x: 4, y: 4, z: 16, core: 2. Of those that a mesh axis runs over, the one named last changes fastest.
Arguments:
- hidden: bfloat16 [24576, 1536], P(('dp', 'tensor')), parts along dimension 0, may hold values from -13 to 13
- norm_gain: bfloat16 [1536], replicated, may hold values from 0.25 to 1.75
- head_weight: bfloat16 [1536, 49152], P(None, 'tensor'), may hold values from -0.45927933 to 0.45927933
- token_order: int32 [24576], P(('dp', 'tensor')), parts along dimension 0, may hold values from 0 to 3071, each once
- targets: int32 [24576], P(('dp', 'tensor')), parts along dimension 0, may hold values from 0 to 49151
- lengths: int32 [64], P('dp'), parts along dimension 0, may hold values from 1 to 768, 3072 in all
Outputs:
- logprob: float32 [24576], P(('dp', 'tensor')), parts along dimension 0
- entropy: float32 [24576], P(('dp', 'tensor')), parts along dimension 0
- seq_logprob: float32 [64], P('dp'), parts along dimension 0
- seq_entropy: float32 [64], P('dp'), parts along dimension 0
The draws below stay inside these ranges and needn't reach their ends.
There are 8 independent parts, one for each index of `dp`. The reference program is written for one: setup_inputs(seed, part) draws one part's arguments, and reference() takes and returns one part's arrays. A program takes and returns all parts, laid end to end along the dimension named above; an argument that names none is the same for every part. Nothing has to cross between parts.
Inputs may be any that keep to these rules, and one draw needn't show every extreme that they name: Each batch's lengths sum to 3072 and the largest is exactly 768.
All inputs are finite; a program needn't handle non-finite values.
Results may differ from the reference program's by a relative error of at most 0.0011.
Values may be sent and summed in bfloat16 or wider, within the bound.
A program may use at most 64 MiB of HBM per device.

```python
import math
import jax
import jax.numpy as jnp
import numpy as np
from jax import lax

D = 1536
V = 49152
TOK_DEV = 48
SEQS = 8
TOKENS = 3072
MOST = 768
N_TENSOR = 64


def draw_hidden(key, part):
    key_noise, key_profile, key_picked, key_strength = jax.random.split(key, 4)
    noise = jax.random.truncated_normal(key_noise, -4.0, 4.0, (TOKENS, D), jnp.float32)
    profile = jax.random.uniform(key_profile, (1, D), jnp.float32, 0.5, 1.5)
    rows = jnp.arange(TOKENS, dtype=jnp.int32)[:, None]
    picked = (jax.random.randint(key_picked, (TOKENS, 1), 0, 8) == 0) | (rows == 0)
    strength = jnp.exp(jax.random.uniform(key_strength, (TOKENS, 1), jnp.float32, math.log(1.5), math.log(6.0)))
    return (noise + jnp.where(picked, strength, 0.0) * profile).astype(jnp.bfloat16)


def draw_head_weight(key, part):
    spread_scale = 3.0 / math.sqrt(D)
    key_base, key_amp, key_columns, key_factor = jax.random.split(key, 4)
    base = jax.random.truncated_normal(key_base, -6.0, 6.0, (D, V), jnp.float32) * spread_scale
    amplitude = jax.random.uniform(key_amp, (4,), jnp.float32, 150.0, 230.0) / D
    factor = jax.random.uniform(key_factor, (D, 4), jnp.float32, 0.9, 1.1)
    first_column = jax.random.randint(key_columns, (4,), 0, V // 2) * 2
    columns = jnp.arange(V, dtype=jnp.int32)[None, :]
    for which_pair in range(4):
        column_profile = factor[:, which_pair:which_pair + 1] * amplitude[which_pair]
        base = jnp.where(columns == first_column[which_pair], column_profile, base)
        base = jnp.where(columns == first_column[which_pair] + 1, column_profile * 0.991, base)
    return base.astype(jnp.bfloat16)


def with_ends(result, key, low, high):
    longest = result.shape.index(max(result.shape))
    spots = []
    for shift in (0, 1):
        where = [jax.random.randint(jax.random.fold_in(key, axis), (), 0, length) for axis, length in enumerate(result.shape)]
        where[longest] = (where[longest] + shift) % result.shape[longest]
        spots.append(tuple(where))
    return result.at[spots[0]].set(low).at[spots[1]].set(high)


def rank_bounds(count, lean):
    portions = [(1 << 20) // math.isqrt(standing ** lean) + 1 for standing in range(1, count + 1)]
    spread = 1 + sum(portions) // (1 << 30)
    return np.cumsum(np.array([max(1, weight // spread) for weight in portions]))


def ranked(rng, extent, number_of, lean):
    table = rank_bounds(number_of, lean)
    ticket = jax.random.randint(jax.random.fold_in(rng, 1), extent, 0, int(table[number_of - 1]))
    rank = jnp.searchsorted(jnp.asarray(table, jnp.int32), ticket, side="right")
    return jax.random.permutation(jax.random.fold_in(rng, 2), number_of)[rank].astype(jnp.int32)


def split_up(number_of, total, most, slope):
    portions = [(1 << 20) // math.isqrt(grade ** slope) + 1 for grade in range(2, number_of + 1)]
    surplus, given = total - most - (number_of - 1), [1] * (number_of - 1)
    while surplus > 0:
        movable = [i for i in range(number_of - 1) if given[i] < most]
        mass, left = sum([portions[i] for i in movable]), surplus
        for i in movable:
            addition = min(most - given[i], max(1, left * portions[i] // mass), surplus)
            given[i] = given[i] + addition
            surplus = surplus - addition
    return np.array([most] + given)


def uneven(rng, amount, total, bound, slope):
    if amount == 2:
        one = jax.random.randint(rng, (), max(1, total - bound), min(bound, total - 1) + 1)
        return jnp.stack([one, total - one])
    sizes = jnp.asarray(split_up(amount, total, bound, slope), jnp.int32)
    twos = (amount - 1) // 2
    source_of, receiver = sizes[1:1 + 2 * twos:2], sizes[2:2 + 2 * twos:2]
    margin = jnp.minimum(source_of - 1, bound - receiver)
    passed = jax.random.randint(jax.random.fold_in(rng, 1), (twos,), 0, 1 << 20) % (margin + 1)
    sizes = sizes.at[1:1 + 2 * twos:2].set(source_of - passed).at[2:2 + 2 * twos:2].set(receiver + passed)
    return sizes[jax.random.permutation(jax.random.fold_in(rng, 2), amount)]


def setup_inputs(seed: int = 0, part: int = 0) -> dict:
    key_list = jax.random.split(jax.random.key(seed), 7)
    own_keys = jax.random.split(jax.random.fold_in(key_list[6], part), 7)
    return {
        "hidden": draw_hidden(jax.random.fold_in(jax.random.fold_in(key_list[6], part), 71), part),
        "norm_gain": jnp.clip(1.0 + 0.15 * jax.random.normal(key_list[1], (D,), jnp.float32), 0.25, 1.75).astype(jnp.bfloat16),
        "head_weight": draw_head_weight(jax.random.fold_in(key_list[6], 71), part),
        "token_order": jax.random.permutation(own_keys[3], TOKENS).astype(jnp.int32),
        "targets": with_ends(ranked(own_keys[4], (TOKENS,), V, 2), jax.random.fold_in(own_keys[4], 3), 0, V - 1).astype(jnp.int32),
        "lengths": uneven(own_keys[5], SEQS, TOKENS, MOST, 2).astype(jnp.int32),
    }


def reference(hidden, norm_gain, head_weight, token_order, targets, lengths):
    values = hidden.astype(jnp.float32)
    scale = lax.rsqrt(lax.optimization_barrier(jnp.mean(values * values, axis=-1, keepdims=True)) + 1e-05)
    normed = (values * scale * norm_gain.astype(jnp.float32)).astype(jnp.bfloat16)
    row_targets = targets[token_order]
    block_rows = normed.reshape(N_TENSOR, TOK_DEV, D)
    block_targets = row_targets.reshape(N_TENSOR, TOK_DEV)

    def one_block(pair):
        rows, wanted = pair
        logits = jnp.dot(rows, head_weight, preferred_element_type=jnp.float32)
        row_peak = lax.optimization_barrier(jnp.max(logits, axis=-1))
        exponent = jnp.exp(logits - row_peak[:, None])
        row_total = lax.optimization_barrier(jnp.sum(exponent, axis=-1))
        row_weighted = lax.optimization_barrier(jnp.sum(exponent * logits, axis=-1))
        columns = jnp.arange(V, dtype=jnp.int32)
        target_logit = lax.optimization_barrier(jnp.sum(jnp.where(columns[None, :] == wanted[:, None], logits, 0.0), axis=-1))
        lse = row_peak + jnp.log(row_total)
        return (target_logit - lse, lse - row_weighted / row_total)
    row_logprob, row_entropy = lax.map(one_block, (block_rows, block_targets))
    row_logprob = row_logprob.reshape(TOKENS)
    row_entropy = row_entropy.reshape(TOKENS)
    logprob = jnp.zeros((TOKENS,), jnp.float32).at[token_order].set(row_logprob)
    entropy = jnp.zeros((TOKENS,), jnp.float32).at[token_order].set(row_entropy)
    starts = jnp.cumsum(lengths) - lengths
    positions = jnp.arange(TOKENS, dtype=jnp.int32)
    member = (positions[:, None] >= starts[None, :]) & (positions[:, None] < (starts + lengths)[None, :])
    counts = lengths.astype(jnp.float32)
    seq_logprob = lax.optimization_barrier(jnp.sum(jnp.where(member, logprob[:, None], 0.0), axis=0)) / counts
    seq_entropy = lax.optimization_barrier(jnp.sum(jnp.where(member, entropy[:, None], 0.0), axis=0)) / counts
    return (logprob, entropy, seq_logprob, seq_entropy)
```

```python
import functools

import jax
import jax.numpy as jnp
from jax import lax
from jax.experimental import pallas as pl
from jax.experimental.pallas import tpu as pltpu
from jax.sharding import PartitionSpec as P

MESH = pl.DeviceIdType.MESH
NX, NY, NZ = 4, 4, 16
NT = NZ * NY
CHUNK = 256
OFFSETS = (NY - 1, 1, 2, 0)


def kernel(
    hid, gain, w_hbm, meta_in, lengths, out,
    xs, wb, lg, meta, thi, tlo, mx, sm, wt, st, stg, fing, fin,
    own_sem, tok_s, tok_r, met_s, met_r, my_s, my_r, wy_s, wy_r, wx_s, wx_r, wp_s, wp_r, b_s, b_r, c_s, c_r,
):
    rows, width = hid.shape
    depth, cols = w_hbm.shape
    per_slice = cols // CHUNK
    seqs = lengths.shape[0]
    dp, tt = lax.axis_index("dp"), lax.axis_index("tensor")
    core, x = lax.rem(dp, 2), lax.div(dp, 2)
    y, z = lax.rem(tt, NY), lax.div(tt, NY)
    q = lax.rem(x, 2)

    def dev(dx=0, dy=0, dz=0, other=False):
        c = 1 - core if other else core
        return (
            lax.rem(x + dx + NX, NX) * 2 + c,
            lax.rem(z + dz + NZ, NZ) * NY + lax.rem(y + dy + NY, NY),
        )

    def send(src, dst, ssem, rsem, device):
        copy = pltpu.make_async_remote_copy(
            src_ref=src, dst_ref=dst, send_sem=ssem, recv_sem=rsem, device_id=device, device_id_type=MESH
        )
        copy.start()
        sent.append(copy)
        return copy

    sent = []
    barrier = pltpu.get_barrier_semaphore()
    friends = [dev(dy=1), dev(dy=-1), dev(dy=2), dev(dz=1), dev(dz=-1), dev(dx=1), dev(dx=-1), dev(other=True)]
    for friend in friends:
        pl.semaphore_signal(barrier, inc=1, device_id=friend, device_id_type=MESH)
    own_copy = pltpu.make_async_copy(w_hbm, wb.at[3], own_sem)
    own_copy.start()
    meta[tt] = meta_in[...]
    values = hid[...].astype(jnp.float32)
    scale = lax.rsqrt(jnp.mean(values * values, axis=-1, keepdims=True) + 1e-05)
    xs[0:rows, :] = (values * scale * gain[...].astype(jnp.float32)).astype(jnp.bfloat16)
    mx[...] = jnp.full(mx.shape, -jnp.inf, jnp.float32)
    sm[...] = jnp.zeros_like(sm)
    wt[...] = jnp.zeros_like(wt)
    thi[...] = jnp.zeros_like(thi)
    tlo[...] = jnp.zeros_like(tlo)
    pl.semaphore_wait(barrier, len(friends))

    def slot(s):
        return xs.at[pl.ds(s * rows, rows), :]

    def send_tokens(k):
        right = send(slot(max(2 * k - 3, 0)), slot(2 * k - 1), tok_s.at[0, k - 1], tok_r.at[0, k - 1], dev(dz=1))
        left = None
        if k < NZ // 2:
            left = send(slot(2 * k - 2), slot(2 * k), tok_s.at[1, k - 1], tok_r.at[1, k - 1], dev(dz=-1))
        return right, left

    def send_meta(k):
        there = meta.at[pl.ds(lax.rem(z - (k - 1) + NZ, NZ) * NY, NY)]
        right = send(there, there, met_s.at[0, k - 1], met_r.at[0, k - 1], dev(dz=1))
        left = None
        if k < NZ // 2:
            there = meta.at[pl.ds(lax.rem(z + (k - 1), NZ) * NY, NY)]
            left = send(there, there, met_s.at[1, k - 1], met_r.at[1, k - 1], dev(dz=-1))
        return right, left

    def row_at(c, parity, e):
        quarter = depth // 4
        return pl.multiple_of(c * (depth // 2) + parity * quarter + e * (quarter // 2), 64)

    def part(r, c, parity, e):
        return wb.at[r, pl.ds(row_at(c, parity, e), depth // 8), :]

    def mine(e):
        return w_hbm.at[pl.ds(row_at(core, q, e), depth // 8), :]

    wy, wx, wp = {}, {}, {}

    def send_y(r, e, src, dy):
        wy[r, e] = send(src, part(r, core, q, e), wy_s.at[r, e], wy_r.at[r, e], dev(dy=dy))

    def got_y(r, e):
        wy[r, e].wait_recv()
        here = part(r, core, q, e)
        if (r, e) == (0, 0):
            send_y(2, 0, here, 1)
        if (r, e) == (1, 1):
            send_y(2, 1, here, -1)
        wx[r, e] = send(here, here, wx_s.at[r, e], wx_r.at[r, e], dev(dx=1 if e == 0 else -1))
        wp[0, r, e] = send(here, here, wp_s.at[0, r, e], wp_r.at[0, r, e], dev(other=True))

    def got_x(r, e):
        wx[r, e].wait_recv()
        here = part(r, core, 1 - q, e)
        wp[1, r, e] = send(here, here, wp_s.at[1, r, e], wp_r.at[1, r, e], dev(other=True))

    def got_partner(r):
        for source in (0, 1):
            for e in (0, 1):
                wp[source, r, e].wait_recv()

    def job(first, count, r_first, r_count):
        here = pl.ds(first, count)

        def step(i, carry):
            j = r_first * per_slice + i
            r, c = lax.div(j, per_slice), lax.rem(j, per_slice)
            block = wb[r, :, pl.ds(pl.multiple_of(c * CHUNK, CHUNK), CHUNK)]
            logits = jnp.dot(xs[here, :], block, preferred_element_type=jnp.float32)
            lg[j, here, :] = logits
            old = mx[here, :]
            peak = jnp.maximum(old, jnp.max(logits, axis=-1, keepdims=True))
            fade = jnp.exp(old - peak)
            exponent = jnp.exp(logits - peak)
            mx[here, :] = peak
            sm[here, :] = sm[here, :] * fade + jnp.sum(exponent, axis=-1, keepdims=True)
            wt[here, :] = wt[here, :] * fade + jnp.sum(exponent * logits, axis=-1, keepdims=True)
            return carry

        lax.fori_loop(0, r_count * per_slice, step, 0)

    tokens = {1: send_tokens(1)}
    metas = {}
    meta_y = [
        send(meta.at[tt], meta.at[tt], my_s.at[i], my_r.at[i], dev(dy=dy)) for i, dy in enumerate((1, -1, 2))
    ]
    send_y(0, 0, mine(0), 1)
    send_y(1, 1, mine(1), -1)
    send_y(0, 1, mine(1), 1)
    send_y(1, 0, mine(0), -1)
    for copy in meta_y:
        copy.wait_recv()
    metas[1] = send_meta(1)

    def ring(k):
        for pair, start in ((tokens, send_tokens), (metas, send_meta)):
            for copy in pair[k]:
                if copy is not None:
                    copy.wait_recv()
            if k < NZ // 2:
                pair[k + 1] = start(k + 1)

    near, mid = 5 * rows, 11 * rows
    total_rows = NZ * rows
    ring(1)
    got_y(0, 0)
    got_y(1, 1)
    ring(2)
    own_copy.wait()
    job(0, near, 3, 1)
    ring(3)
    got_y(0, 1)
    got_y(1, 0)
    got_x(0, 0)
    got_x(1, 1)
    ring(4)
    ring(5)
    job(near, mid - near, 3, 1)
    got_y(2, 0)
    got_y(2, 1)
    got_x(0, 1)
    got_x(1, 0)
    ring(6)
    got_partner(0)
    got_partner(1)
    job(0, mid, 0, 2)
    ring(7)
    got_x(2, 0)
    got_x(2, 1)
    got_partner(2)
    job(0, mid, 2, 1)
    ring(8)
    job(mid, total_rows - mid, 0, 4)

    lane = lax.broadcasted_iota(jnp.int32, (rows, 128), 1)
    eye = lane == lax.broadcasted_iota(jnp.int32, (rows, 128), 0)
    for t in range(NT):
        ids = meta[t, 1:2, :]
        high = ids >> 8
        thi[t:t + 1, :] = high.astype(jnp.float32)
        tlo[t:t + 1, :] = (ids - (high << 8)).astype(jnp.float32)
    high_ids, low_ids = thi[...].astype(jnp.bfloat16), tlo[...].astype(jnp.bfloat16)
    lane_chunk = lax.broadcasted_iota(jnp.int32, (rows, CHUNK), 1)

    def to_row(column):
        return jnp.sum(jnp.where(eye, column, 0.0), axis=0, keepdims=True)

    stats = []

    def send_stats(s):
        k = (s + 1) // 2
        if s % 2:
            theirs, dz = (2 * k if k < NZ // 2 else s), -k
        else:
            theirs, dz = 2 * k - 1, k
        stats.append(send(st.at[s], stg.at[theirs], b_s.at[s], b_r.at[theirs], dev(dz=dz)))

    for s in range(NZ - 1, -1, -1):
        k = (s + 1) // 2
        zs = lax.rem(z + (-k if s % 2 else k) + NZ, NZ)
        order = meta[zs * NY + y, 0:1, :]
        order = jnp.sum(jnp.where(eye, order.astype(jnp.float32), 0.0), axis=1, keepdims=True).astype(jnp.int32)
        inside = (order >= lane * rows) & (order < lane * rows + rows)
        picked = jnp.where(inside, 1.0, 0.0).astype(jnp.bfloat16)
        ids = 256.0 * jnp.dot(picked, high_ids, preferred_element_type=jnp.float32) + jnp.dot(
            picked, low_ids, preferred_element_type=jnp.float32
        )
        start = jnp.sum(jnp.where(inside, (lane * rows).astype(jnp.float32), 0.0), axis=1, keepdims=True)
        wanted = jnp.sum(
            jnp.where(lane == order - start.astype(jnp.int32), ids, 0.0), axis=1, keepdims=True
        ).astype(jnp.int32)
        found = jnp.zeros((rows, CHUNK), jnp.float32)
        for j in range(4 * per_slice):
            base = (z * NY + lax.rem(y + OFFSETS[j // per_slice], NY)) * cols + (j % per_slice) * CHUNK
            found += jnp.where(lane_chunk == wanted - base, lg[j, s * rows:(s + 1) * rows, :], 0.0)
        target = jnp.sum(found, axis=-1, keepdims=True)
        here = slice(s * rows, (s + 1) * rows)
        place = stg if s == 0 else st
        place[s, 0:1, :] = to_row(mx[here, :])
        place[s, 1:2, :] = to_row(sm[here, :])
        place[s, 2:3, :] = to_row(wt[here, :])
        place[s, 3:4, :] = to_row(target)
        if s + 1 < NZ:
            send_stats(s + 1)

    for copy in stats:
        copy.wait_recv()
    peak = stg[0, 0:1, :]
    for s in range(1, NZ):
        peak = jnp.maximum(peak, stg[s, 0:1, :])
    row_total = jnp.zeros((1, 128), jnp.float32)
    row_weighted, target_logit = row_total, row_total
    for s in range(NZ):
        fade = jnp.exp(stg[s, 0:1, :] - peak)
        row_total += stg[s, 1:2, :] * fade
        row_weighted += stg[s, 2:3, :] * fade
        target_logit += stg[s, 3:4, :]
    row_total = jnp.where(lane[0:1, :] < rows, row_total, 1.0)
    lse = peak + jnp.log(row_total)
    fing[0:1, :] = target_logit - lse
    fing[1:2, :] = lse - row_weighted / row_total
    fin[tt] = fing[...]

    def final_copy(i):
        other = lax.rem(tt + i, NT)
        return pltpu.make_async_remote_copy(
            src_ref=fing, dst_ref=fin.at[tt], send_sem=c_s.at[i], recv_sem=c_r.at[i],
            device_id=(dp, other), device_id_type=MESH,
        )

    def start_final(i, carry):
        final_copy(i).start()
        return carry

    lax.fori_loop(1, NT, start_final, 0)
    sub8 = lax.broadcasted_iota(jnp.int32, (seqs, 128), 0)
    lane8 = lax.broadcasted_iota(jnp.int32, (seqs, 128), 1)
    first = jnp.zeros((seqs, 128), jnp.int32)
    last = first
    running = jnp.int32(0)
    for i in range(seqs):
        first = jnp.where(sub8 == i, running, first)
        running = running + lengths[i]
        last = jnp.where(sub8 == i, running, last)
    for copy in sent:
        copy.wait_send()

    def end_final(i, carry):
        final_copy(i).wait()
        return carry

    lax.fori_loop(1, NT, end_final, 0)
    position = tt * rows + lax.broadcasted_iota(jnp.int32, (rows, 128), 0)

    def place_rows(t, carry):
        logprob, entropy, seq_logprob, seq_entropy = carry
        order = meta[t, 0:1, :]
        got_logprob, got_entropy = fin[t, 0:1, :], fin[t, 1:2, :]
        match = order == position
        member = (order >= first) & (order < last)
        return (
            logprob + jnp.where(match, got_logprob, 0.0),
            entropy + jnp.where(match, got_entropy, 0.0),
            seq_logprob + jnp.where(member, got_logprob, 0.0),
            seq_entropy + jnp.where(member, got_entropy, 0.0),
        )

    wide, narrow = jnp.zeros((rows, 128), jnp.float32), jnp.zeros((seqs, 128), jnp.float32)
    logprob, entropy, seq_logprob, seq_entropy = lax.fori_loop(0, NT, place_rows, (wide, wide, narrow, narrow))
    out[...] = jnp.zeros_like(out)
    out[0:1, :] = to_row(jnp.sum(logprob, axis=1, keepdims=True))
    out[1:2, :] = to_row(jnp.sum(entropy, axis=1, keepdims=True))
    counts = (last - first).astype(jnp.float32)
    for i, value in ((2, seq_logprob), (3, seq_entropy)):
        mean = jnp.sum(value, axis=1, keepdims=True) / counts
        out[i:i + 1, :] = jnp.sum(jnp.where(sub8 == lane8, mean, 0.0), axis=0, keepdims=True)


def per_device(hidden, norm_gain, head_weight, token_order, targets, lengths):
    rows, width = hidden.shape
    depth, cols = head_weight.shape
    seqs = lengths.shape[0]
    meta = jnp.stack([
        jnp.pad(token_order, (0, 128 - rows), constant_values=-1),
        jnp.pad(targets, (0, 128 - rows)),
    ])
    total = NZ * rows
    vmem, dma = pltpu.VMEM, pltpu.SemaphoreType.DMA
    half = NZ // 2
    in_vmem = pl.BlockSpec(memory_space=pltpu.VMEM)
    out = pl.pallas_call(
        kernel,
        out_shape=jax.ShapeDtypeStruct((8, 128), jnp.float32),
        in_specs=[
            in_vmem, in_vmem, pl.BlockSpec(memory_space=pl.ANY), in_vmem, pl.BlockSpec(memory_space=pltpu.SMEM),
        ],
        out_specs=in_vmem,
        scratch_shapes=[
            vmem((total, width), jnp.bfloat16),
            vmem((4, depth, cols), jnp.bfloat16),
            vmem((4 * cols // CHUNK, total, CHUNK), jnp.float32),
            vmem((NT, 2, 128), jnp.int32),
            vmem((128, 128), jnp.float32),
            vmem((128, 128), jnp.float32),
            vmem((total, 1), jnp.float32),
            vmem((total, 1), jnp.float32),
            vmem((total, 1), jnp.float32),
            vmem((NZ, 4, 128), jnp.float32),
            vmem((NZ, 4, 128), jnp.float32),
            vmem((2, 128), jnp.float32),
            vmem((NT, 2, 128), jnp.float32),
            dma,
            dma((2, half)), dma((2, half)),
            dma((2, half)), dma((2, half)),
            dma((3,)), dma((3,)),
            dma((3, 2)), dma((3, 2)),
            dma((3, 2)), dma((3, 2)),
            dma((2, 3, 2)), dma((2, 3, 2)),
            dma((NZ,)), dma((NZ,)),
            dma((NT,)), dma((NT,)),
        ],
        compiler_params=pltpu.CompilerParams(
            collective_id=0, has_side_effects=True, vmem_limit_bytes=60 * 1024 * 1024
        ),
    )(hidden, norm_gain.reshape(1, width), head_weight, meta, lengths)
    return out[0, :rows], out[1, :rows], out[2, :seqs], out[3, :seqs]


def solution(mesh):
    return jax.shard_map(
        per_device,
        mesh=mesh,
        in_specs=(
            P(("dp", "tensor"), None),
            P(),
            P(None, "tensor"),
            P(("dp", "tensor")),
            P(("dp", "tensor")),
            P("dp"),
        ),
        out_specs=(P(("dp", "tensor")), P(("dp", "tensor")), P("dp"), P("dp")),
        check_vma=False,
    )
```

```python
import functools

import jax
import jax.numpy as jnp
from jax import lax
from jax.experimental import pallas as pl
from jax.experimental.pallas import tpu as pltpu
from jax.sharding import PartitionSpec as P

MESH = pl.DeviceIdType.MESH
NX, NY, NZ = 4, 4, 16
NT = NZ * NY
PIECE = 16
OFFSETS = (NY - 1, 1, 2, 0)


def kernel(
    hid, gain, w_hbm, order_in, target_in, lengths, out_logprob, out_entropy, out_seq_logprob, out_seq_entropy,
    xs, wb, lg, meta, thi, tlo, mx, sm, wt, st, stg, fing, fin,
    own_sem, tok_s, tok_r, met_s, met_r, my_s, my_r, wy_s, wy_r, wx_s, wx_r, wp_s, wp_r, b_s, b_r, c_s, c_r,
):
    rows, width = hid.shape
    depth, cols = w_hbm.shape
    seqs = lengths.shape[0]
    dp, tt = lax.axis_index("dp"), lax.axis_index("tensor")
    core, x = lax.rem(dp, 2), lax.div(dp, 2)
    y, z = lax.rem(tt, NY), lax.div(tt, NY)
    q = lax.rem(x, 2)

    def dev(dx=0, dy=0, dz=0, other=False):
        c = 1 - core if other else core
        return (
            lax.rem(x + dx + NX, NX) * 2 + c,
            lax.rem(z + dz + NZ, NZ) * NY + lax.rem(y + dy + NY, NY),
        )

    def send(src, dst, ssem, rsem, device):
        copy = pltpu.make_async_remote_copy(
            src_ref=src, dst_ref=dst, send_sem=ssem, recv_sem=rsem, device_id=device, device_id_type=MESH
        )
        copy.start()
        sent.append(copy)
        return copy

    sent = []
    barrier = pltpu.get_barrier_semaphore()
    friends = [dev(dy=1), dev(dy=-1), dev(dy=2), dev(dz=1), dev(dz=-1), dev(dx=1), dev(dx=-1), dev(other=True)]
    for friend in friends:
        pl.semaphore_signal(barrier, inc=1, device_id=friend, device_id_type=MESH)
    own_copy = pltpu.make_async_copy(w_hbm, wb.at[3], own_sem)
    own_copy.start()
    meta[tt, 0:1, :] = jnp.full((1, 128), -1, jnp.int32)
    meta[tt, 1:2, :] = jnp.zeros((1, 128), jnp.int32)
    meta[tt, 0:1, 0:rows] = order_in[...].reshape(1, rows)
    meta[tt, 1:2, 0:rows] = target_in[...].reshape(1, rows)
    values = hid[...].astype(jnp.float32)
    scale = lax.rsqrt(jnp.mean(values * values, axis=-1, keepdims=True) + 1e-05)
    xs[0:rows, :] = (values * scale * gain[...].astype(jnp.float32).reshape(1, width)).astype(jnp.bfloat16)
    mx[...] = jnp.full(mx.shape, -jnp.inf, jnp.float32)
    sm[...] = jnp.zeros_like(sm)
    wt[...] = jnp.zeros_like(wt)
    thi[...] = jnp.zeros_like(thi)
    tlo[...] = jnp.zeros_like(tlo)
    pl.semaphore_wait(barrier, len(friends))

    def slot(s, piece):
        return xs.at[pl.ds(s * rows + piece * PIECE, PIECE), :]

    def send_tokens(k, piece):
        def one(way, source, target, dz):
            where = way, k - 1, piece
            return send(slot(source, piece), slot(target, piece), tok_s.at[where], tok_r.at[where], dev(dz=dz))

        right = one(0, max(2 * k - 3, 0), 2 * k - 1, 1)
        return (right, one(1, 2 * k - 2, 2 * k, -1)) if k < NZ // 2 else (right,)

    def send_meta(k):
        there = meta.at[pl.ds(lax.rem(z - (k - 1) + NZ, NZ) * NY, NY)]
        right = send(there, there, met_s.at[0, k - 1], met_r.at[0, k - 1], dev(dz=1))
        left = None
        if k < NZ // 2:
            there = meta.at[pl.ds(lax.rem(z + (k - 1), NZ) * NY, NY)]
            left = send(there, there, met_s.at[1, k - 1], met_r.at[1, k - 1], dev(dz=-1))
        return right, left

    def row_at(c, parity, e):
        quarter = depth // 4
        return pl.multiple_of(c * (depth // 2) + parity * quarter + e * (quarter // 2), 64)

    def part(r, c, parity, e):
        return wb.at[r, pl.ds(row_at(c, parity, e), depth // 8), :]

    def mine(e):
        return w_hbm.at[pl.ds(row_at(core, q, e), depth // 8), :]

    wy, wx, wp = {}, {}, {}

    def send_y(r, e, src, dy):
        wy[r, e] = send(src, part(r, core, q, e), wy_s.at[r, e], wy_r.at[r, e], dev(dy=dy))

    def got_y(r, e):
        wy[r, e].wait_recv()
        here = part(r, core, q, e)
        if (r, e) == (0, 0):
            send_y(2, 0, here, 1)
        if (r, e) == (1, 1):
            send_y(2, 1, here, -1)
        wx[r, e] = send(here, here, wx_s.at[r, e], wx_r.at[r, e], dev(dx=1 if e == 0 else -1))
        wp[0, r, e] = send(here, here, wp_s.at[0, r, e], wp_r.at[0, r, e], dev(other=True))

    def got_x(r, e):
        wx[r, e].wait_recv()
        here = part(r, core, 1 - q, e)
        wp[1, r, e] = send(here, here, wp_s.at[1, r, e], wp_r.at[1, r, e], dev(other=True))

    def got_partner(r):
        for source in (0, 1):
            for e in (0, 1):
                wp[source, r, e].wait_recv()

    def job(first, count, r_first, r_count):
        here = pl.ds(first, count)

        def step(i, carry):
            r = r_first + i
            logits = jnp.dot(xs[here, :], wb[r], preferred_element_type=jnp.float32)
            parts = [logits[:, c:c + 128] for c in range(0, cols, 128)]
            lg[r, here, :] = logits
            old = mx[here, :]
            peak = functools.reduce(jnp.maximum, parts, old)
            fade = jnp.exp(old - peak)
            total, weighted = sm[here, :] * fade, wt[here, :] * fade
            for piece in parts:
                exponent = jnp.exp(piece - peak)
                total += exponent
                weighted += exponent * piece
            mx[here, :], sm[here, :], wt[here, :] = peak, total, weighted
            return carry

        lax.fori_loop(0, r_count, step, 0)

    pieces = rows // PIECE
    tokens = {(1, piece): send_tokens(1, piece) for piece in range(pieces)}
    metas = {}
    meta_y = [
        send(meta.at[tt], meta.at[tt], my_s.at[i], my_r.at[i], dev(dy=dy)) for i, dy in enumerate((1, -1, 2))
    ]
    send_y(0, 0, mine(0), 1)
    send_y(1, 1, mine(1), -1)
    send_y(0, 1, mine(1), 1)
    send_y(1, 0, mine(0), -1)
    for copy in meta_y:
        copy.wait_recv()
    metas[1] = send_meta(1)

    def ring(k):
        for copy in metas[k]:
            if copy is not None:
                copy.wait_recv()
        if k < NZ // 2:
            metas[k + 1] = send_meta(k + 1)
        for piece in range(pieces):
            for copy in tokens[k, piece]:
                copy.wait_recv()
            if k < NZ // 2:
                tokens[k + 1, piece] = send_tokens(k + 1, piece)

    near, mid = 5 * rows, 11 * rows
    total_rows = NZ * rows
    ring(1)
    got_y(0, 0)
    got_y(1, 1)
    ring(2)
    own_copy.wait()
    job(0, near, 3, 1)
    ring(3)
    got_y(0, 1)
    got_y(1, 0)
    got_x(0, 0)
    got_x(1, 1)
    ring(4)
    ring(5)
    job(near, mid - near, 3, 1)
    got_y(2, 0)
    got_y(2, 1)
    got_x(0, 1)
    got_x(1, 0)
    ring(6)
    got_partner(0)
    got_partner(1)
    job(0, mid, 0, 2)
    ring(7)
    got_x(2, 0)
    got_x(2, 1)
    got_partner(2)
    job(0, mid, 2, 1)
    ring(8)
    job(mid, total_rows - mid, 0, 4)

    lane = lax.broadcasted_iota(jnp.int32, (rows, 128), 1)
    eye = lane == lax.broadcasted_iota(jnp.int32, (rows, 128), 0)
    for t in range(NT):
        ids = meta[t, 1:2, :]
        high = ids >> 8
        thi[t:t + 1, :] = high.astype(jnp.float32)
        tlo[t:t + 1, :] = (ids - (high << 8)).astype(jnp.float32)
    high_ids, low_ids = thi[...].astype(jnp.bfloat16), tlo[...].astype(jnp.bfloat16)

    def to_row(column):
        return jnp.sum(jnp.where(eye, column, 0.0), axis=0, keepdims=True)

    stats = []

    def send_stats(s):
        k = (s + 1) // 2
        if s % 2:
            theirs, dz = (2 * k if k < NZ // 2 else s), -k
        else:
            theirs, dz = 2 * k - 1, k
        stats.append(send(st.at[s], stg.at[theirs], b_s.at[s], b_r.at[theirs], dev(dz=dz)))

    for s in range(NZ - 1, -1, -1):
        k = (s + 1) // 2
        zs = lax.rem(z + (-k if s % 2 else k) + NZ, NZ)
        order = meta[zs * NY + y, 0:1, :]
        order = jnp.sum(jnp.where(eye, order.astype(jnp.float32), 0.0), axis=1, keepdims=True).astype(jnp.int32)
        inside = (order >= lane * rows) & (order < lane * rows + rows)
        picked = jnp.where(inside, 1.0, 0.0).astype(jnp.bfloat16)
        ids = 256.0 * jnp.dot(picked, high_ids, preferred_element_type=jnp.float32) + jnp.dot(
            picked, low_ids, preferred_element_type=jnp.float32
        )
        start = jnp.sum(jnp.where(inside, (lane * rows).astype(jnp.float32), 0.0), axis=1, keepdims=True)
        wanted = jnp.sum(
            jnp.where(lane == order - start.astype(jnp.int32), ids, 0.0), axis=1, keepdims=True
        ).astype(jnp.int32)
        here = slice(s * rows, (s + 1) * rows)
        found = jnp.zeros((rows, 128), jnp.float32)
        for r in range(4):
            near_wanted = wanted - (z * NY + lax.rem(y + OFFSETS[r], NY)) * cols
            for c in range(0, cols, 128):
                found += jnp.where(lane == near_wanted - c, lg[r, here, c:c + 128], 0.0)
        target = jnp.sum(found, axis=-1, keepdims=True)
        lane_peak = mx[here, :]
        peak = jnp.max(lane_peak, axis=-1, keepdims=True)
        fade = jnp.exp(lane_peak - peak)
        place = stg if s == 0 else st
        place[s, 0:1, :] = to_row(peak)
        place[s, 1:2, :] = to_row(jnp.sum(sm[here, :] * fade, axis=-1, keepdims=True))
        place[s, 2:3, :] = to_row(jnp.sum(wt[here, :] * fade, axis=-1, keepdims=True))
        place[s, 3:4, :] = to_row(target)
        if s + 1 < NZ:
            send_stats(s + 1)

    for copy in stats:
        copy.wait_recv()
    peak = stg[0, 0:1, :]
    for s in range(1, NZ):
        peak = jnp.maximum(peak, stg[s, 0:1, :])
    row_total = jnp.zeros((1, 128), jnp.float32)
    row_weighted, target_logit = row_total, row_total
    for s in range(NZ):
        fade = jnp.exp(stg[s, 0:1, :] - peak)
        row_total += stg[s, 1:2, :] * fade
        row_weighted += stg[s, 2:3, :] * fade
        target_logit += stg[s, 3:4, :]
    row_total = jnp.where(lane[0:1, :] < rows, row_total, 1.0)
    lse = peak + jnp.log(row_total)
    fing[0:1, :] = target_logit - lse
    fing[1:2, :] = lse - row_weighted / row_total
    fin[tt] = fing[...]

    def final_copy(i):
        other = lax.rem(tt + i, NT)
        return pltpu.make_async_remote_copy(
            src_ref=fing, dst_ref=fin.at[tt], send_sem=c_s.at[i], recv_sem=c_r.at[i],
            device_id=(dp, other), device_id_type=MESH,
        )

    def start_final(i, carry):
        final_copy(i).start()
        return carry

    lax.fori_loop(1, NT, start_final, 0)
    sub8 = lax.broadcasted_iota(jnp.int32, (seqs, 128), 0)
    lane8 = lax.broadcasted_iota(jnp.int32, (seqs, 128), 1)
    first = jnp.zeros((seqs, 128), jnp.int32)
    last = first
    running = jnp.int32(0)
    for i in range(seqs):
        first = jnp.where(sub8 == i, running, first)
        running = running + lengths[i]
        last = jnp.where(sub8 == i, running, last)
    for copy in sent:
        copy.wait_send()

    def end_final(i, carry):
        final_copy(i).wait()
        return carry

    lax.fori_loop(1, NT, end_final, 0)
    position = tt * rows + lax.broadcasted_iota(jnp.int32, (rows, 128), 0)

    def place_rows(t, carry):
        logprob, entropy, seq_logprob, seq_entropy = carry
        order = meta[t, 0:1, :]
        got_logprob, got_entropy = fin[t, 0:1, :], fin[t, 1:2, :]
        match = order == position
        member = (order >= first) & (order < last)
        return (
            logprob + jnp.where(match, got_logprob, 0.0),
            entropy + jnp.where(match, got_entropy, 0.0),
            seq_logprob + jnp.where(member, got_logprob, 0.0),
            seq_entropy + jnp.where(member, got_entropy, 0.0),
        )

    wide, narrow = jnp.zeros((rows, 128), jnp.float32), jnp.zeros((seqs, 128), jnp.float32)
    logprob, entropy, seq_logprob, seq_entropy = lax.fori_loop(0, NT, place_rows, (wide, wide, narrow, narrow))
    out_logprob[...] = to_row(jnp.sum(logprob, axis=1, keepdims=True))[0, :rows]
    out_entropy[...] = to_row(jnp.sum(entropy, axis=1, keepdims=True))[0, :rows]
    counts = (last - first).astype(jnp.float32)
    for ref, value in ((out_seq_logprob, seq_logprob), (out_seq_entropy, seq_entropy)):
        mean = jnp.sum(value, axis=1, keepdims=True) / counts
        ref[...] = jnp.sum(jnp.where(sub8 == lane8, mean, 0.0), axis=0, keepdims=True)[0, :seqs]


def per_device(hidden, norm_gain, head_weight, token_order, targets, lengths):
    rows, width = hidden.shape
    depth, cols = head_weight.shape
    seqs = lengths.shape[0]
    total = NZ * rows
    vmem, dma = pltpu.VMEM, pltpu.SemaphoreType.DMA
    half = NZ // 2
    in_vmem = pl.BlockSpec(memory_space=pltpu.VMEM)
    return pl.pallas_call(
        kernel,
        out_shape=[jax.ShapeDtypeStruct((n,), jnp.float32) for n in (rows, rows, seqs, seqs)],
        in_specs=[
            in_vmem, in_vmem, pl.BlockSpec(memory_space=pl.ANY), in_vmem, in_vmem,
            pl.BlockSpec(memory_space=pltpu.SMEM),
        ],
        out_specs=[in_vmem] * 4,
        scratch_shapes=[
            vmem((total, width), jnp.bfloat16),
            vmem((4, depth, cols), jnp.bfloat16),
            vmem((4, total, cols), jnp.float32),
            vmem((NT, 2, 128), jnp.int32),
            vmem((128, 128), jnp.float32),
            vmem((128, 128), jnp.float32),
            vmem((total, 128), jnp.float32),
            vmem((total, 128), jnp.float32),
            vmem((total, 128), jnp.float32),
            vmem((NZ, 4, 128), jnp.float32),
            vmem((NZ, 4, 128), jnp.float32),
            vmem((2, 128), jnp.float32),
            vmem((NT, 2, 128), jnp.float32),
            dma,
            dma((2, half, rows // PIECE)), dma((2, half, rows // PIECE)),
            dma((2, half)), dma((2, half)),
            dma((3,)), dma((3,)),
            dma((3, 2)), dma((3, 2)),
            dma((3, 2)), dma((3, 2)),
            dma((2, 3, 2)), dma((2, 3, 2)),
            dma((NZ,)), dma((NZ,)),
            dma((NT,)), dma((NT,)),
        ],
        compiler_params=pltpu.CompilerParams(
            collective_id=0, has_side_effects=True, vmem_limit_bytes=60 * 1024 * 1024
        ),
    )(hidden, norm_gain, head_weight, token_order, targets, lengths)


def solution(mesh):
    return jax.shard_map(
        per_device,
        mesh=mesh,
        in_specs=(
            P(("dp", "tensor"), None),
            P(),
            P(None, "tensor"),
            P(("dp", "tensor")),
            P(("dp", "tensor")),
            P("dp"),
        ),
        out_specs=(P(("dp", "tensor")), P(("dp", "tensor")), P("dp"), P("dp")),
        check_vma=False,
    )
```

```python
import functools

import jax
import jax.numpy as jnp
from jax import lax
from jax.experimental import pallas as pl
from jax.experimental.pallas import tpu as pltpu
from jax.sharding import PartitionSpec as P

MESH = pl.DeviceIdType.MESH
NX, NY, NZ = 4, 4, 16
NT = NZ * NY
PIECE = 16
OFFSETS = (NY - 1, 1, 2, 0)


def kernel(
    hid_in, gain_in, w_hbm, order_in, target_in, lengths_in, out,
    hid, gain, order_own, target_own, lengths, in_sem, xs, wb, lg, meta, thi, tlo, mx, sm, wt, st, stg, fing, fin,
    own_sem, tok_s, tok_r, met_s, met_r, my_s, my_r, wy_s, wy_r, wx_s, wx_r, wp_s, wp_r, b_s, b_r, c_s, c_r,
):
    rows, width = hid_in.shape
    depth, cols = w_hbm.shape
    seqs = lengths_in.shape[0]
    dp, tt = lax.axis_index("dp"), lax.axis_index("tensor")
    core, x = lax.rem(dp, 2), lax.div(dp, 2)
    y, z = lax.rem(tt, NY), lax.div(tt, NY)
    q = lax.rem(x, 2)

    def dev(dx=0, dy=0, dz=0, other=False):
        c = 1 - core if other else core
        return (
            lax.rem(x + dx + NX, NX) * 2 + c,
            lax.rem(z + dz + NZ, NZ) * NY + lax.rem(y + dy + NY, NY),
        )

    def send(src, dst, ssem, rsem, device):
        copy = pltpu.make_async_remote_copy(
            src_ref=src, dst_ref=dst, send_sem=ssem, recv_sem=rsem, device_id=device, device_id_type=MESH
        )
        copy.start()
        sent.append(copy)
        return copy

    sent = []
    barrier = pltpu.get_barrier_semaphore()
    friends = [dev(dy=1), dev(dy=-1), dev(dy=2), dev(dz=1), dev(dz=-1), dev(dx=1), dev(dx=-1), dev(other=True)]
    for friend in friends:
        pl.semaphore_signal(barrier, inc=1, device_id=friend, device_id_type=MESH)
    own_copy = pltpu.make_async_copy(w_hbm, wb.at[3], own_sem)
    inputs = [
        pltpu.make_async_copy(source, target, in_sem.at[i])
        for i, (source, target) in enumerate((
            (hid_in, hid), (gain_in, gain), (order_in, order_own), (target_in, target_own), (lengths_in, lengths),
        ))
    ]
    for copy in inputs:
        copy.start()
    own_copy.start()
    for copy in inputs:
        copy.wait()
    meta[tt, 0:1, :] = jnp.full((1, 128), -1, jnp.int32)
    meta[tt, 1:2, :] = jnp.zeros((1, 128), jnp.int32)
    meta[tt, 0:1, 0:rows] = order_own[...].reshape(1, rows)
    meta[tt, 1:2, 0:rows] = target_own[...].reshape(1, rows)
    values = hid[...].astype(jnp.float32)
    scale = lax.rsqrt(jnp.mean(values * values, axis=-1, keepdims=True) + 1e-05)
    xs[0:rows, :] = (values * scale * gain[...].astype(jnp.float32).reshape(1, width)).astype(jnp.bfloat16)
    mx[...] = jnp.full(mx.shape, -jnp.inf, jnp.float32)
    sm[...] = jnp.zeros_like(sm)
    wt[...] = jnp.zeros_like(wt)
    thi[...] = jnp.zeros_like(thi)
    tlo[...] = jnp.zeros_like(tlo)
    pl.semaphore_wait(barrier, len(friends))

    def slot(s, piece):
        return xs.at[pl.ds(s * rows + piece * PIECE, PIECE), :]

    def send_tokens(k, piece):
        def one(way, source, target, dz):
            where = way, k - 1, piece
            return send(slot(source, piece), slot(target, piece), tok_s.at[where], tok_r.at[where], dev(dz=dz))

        if k == NZ // 2:
            return (one(piece % 2, 2 * k - 3 + piece % 2, 2 * k - 1, 1 - 2 * (piece % 2)),)
        right = one(0, max(2 * k - 3, 0), 2 * k - 1, 1)
        return right, one(1, 2 * k - 2, 2 * k, -1)

    def send_meta(k):
        there = meta.at[pl.ds(lax.rem(z - (k - 1) + NZ, NZ) * NY, NY)]
        right = send(there, there, met_s.at[0, k - 1], met_r.at[0, k - 1], dev(dz=1))
        left = None
        if k < NZ // 2:
            there = meta.at[pl.ds(lax.rem(z + (k - 1), NZ) * NY, NY)]
            left = send(there, there, met_s.at[1, k - 1], met_r.at[1, k - 1], dev(dz=-1))
        return right, left

    def row_at(c, parity, e):
        quarter = depth // 4
        return pl.multiple_of(c * (depth // 2) + parity * quarter + e * (quarter // 2), 64)

    def part(r, c, parity, e):
        return wb.at[r, pl.ds(row_at(c, parity, e), depth // 8), :]

    def mine(e):
        return w_hbm.at[pl.ds(row_at(core, q, e), depth // 8), :]

    wy, wx, wp = {}, {}, {}

    def send_y(r, e, src, dy):
        wy[r, e] = send(src, part(r, core, q, e), wy_s.at[r, e], wy_r.at[r, e], dev(dy=dy))

    def got_y(r, e):
        wy[r, e].wait_recv()
        here = part(r, core, q, e)
        if (r, e) == (0, 0):
            send_y(2, 0, here, 1)
        if (r, e) == (1, 1):
            send_y(2, 1, here, -1)
        wx[r, e] = send(here, here, wx_s.at[r, e], wx_r.at[r, e], dev(dx=1 if e == 0 else -1))
        wp[0, r, e] = send(here, here, wp_s.at[0, r, e], wp_r.at[0, r, e], dev(other=True))

    def got_x(r, e):
        wx[r, e].wait_recv()
        here = part(r, core, 1 - q, e)
        wp[1, r, e] = send(here, here, wp_s.at[1, r, e], wp_r.at[1, r, e], dev(other=True))

    def got_partner(r):
        for source in (0, 1):
            for e in (0, 1):
                wp[source, r, e].wait_recv()

    def job(first, count, r_first, r_count):
        here = pl.ds(first, count)

        def step(i, carry):
            r = lax.rem(r_first + i, 4)
            logits = jnp.dot(xs[here, :], wb[r], preferred_element_type=jnp.float32)
            parts = [logits[:, c:c + 128] for c in range(0, cols, 128)]
            lg[r, here, :] = logits
            old = mx[here, :]
            peak = functools.reduce(jnp.maximum, parts, old)
            fade = jnp.exp(old - peak)
            total, weighted = sm[here, :] * fade, wt[here, :] * fade
            for piece in parts:
                exponent = jnp.exp(piece - peak)
                total += exponent
                weighted += exponent * piece
            mx[here, :], sm[here, :], wt[here, :] = peak, total, weighted
            return carry

        lax.fori_loop(0, r_count, step, 0)

    pieces = rows // PIECE
    tokens = {(1, piece): send_tokens(1, piece) for piece in range(pieces)}
    metas = {}
    meta_y = [
        send(meta.at[tt], meta.at[tt], my_s.at[i], my_r.at[i], dev(dy=dy)) for i, dy in enumerate((1, -1, 2))
    ]
    send_y(0, 0, mine(0), 1)
    send_y(1, 1, mine(1), -1)
    send_y(0, 1, mine(1), 1)
    send_y(1, 0, mine(0), -1)
    for copy in meta_y:
        copy.wait_recv()
    metas[1] = send_meta(1)

    def ring_meta(k):
        for copy in metas[k]:
            if copy is not None:
                copy.wait_recv()
        if k < NZ // 2:
            metas[k + 1] = send_meta(k + 1)

    def ring_rows(k):
        for piece in range(pieces):
            for copy in tokens[k, piece]:
                copy.wait_recv()
            if k < NZ // 2:
                tokens[k + 1, piece] = send_tokens(k + 1, piece)

    def ring(k):
        ring_meta(k)
        ring_rows(k)

    near, mid, far = 5 * rows, 9 * rows, 13 * rows
    ring(1)
    got_y(0, 0)
    got_y(1, 1)
    ring(2)
    own_copy.wait()
    job(0, near, 3, 1)
    ring(3)
    got_y(0, 1)
    got_y(1, 0)
    got_x(0, 0)
    got_x(1, 1)
    ring(4)
    got_y(2, 0)
    got_y(2, 1)
    got_x(0, 1)
    got_x(1, 0)
    job(near, mid - near, 3, 1)
    ring(5)
    got_partner(0)
    got_partner(1)
    job(0, mid, 0, 1)
    ring(6)
    got_x(2, 0)
    got_x(2, 1)
    job(0, mid, 1, 1)
    job(mid, far - mid, 3, 3)
    ring(7)
    got_partner(2)
    job(0, far, 2, 1)
    ring_meta(8)

    lane = lax.broadcasted_iota(jnp.int32, (rows, 128), 1)
    eye = lane == lax.broadcasted_iota(jnp.int32, (rows, 128), 0)
    for t in range(NT):
        ids = meta[t, 1:2, :]
        high = ids >> 8
        thi[t:t + 1, :] = high.astype(jnp.float32)
        tlo[t:t + 1, :] = (ids - (high << 8)).astype(jnp.float32)
    high_ids, low_ids = thi[...].astype(jnp.bfloat16), tlo[...].astype(jnp.bfloat16)

    def to_row(column):
        return jnp.sum(jnp.where(eye, column, 0.0), axis=0, keepdims=True)

    stats = []

    def send_stats(s):
        k = (s + 1) // 2
        if s % 2:
            theirs, dz = (2 * k if k < NZ // 2 else s), -k
        else:
            theirs, dz = 2 * k - 1, k
        stats.append(send(st.at[s], stg.at[theirs], b_s.at[s], b_r.at[theirs], dev(dz=dz)))

    def finish_all(first, count):
        slots, here = range(first, first + count), pl.ds(first * rows, count * rows)
        orders = []
        for s in slots:
            k = (s + 1) // 2
            zs = lax.rem(z + (-k if s % 2 else k) + NZ, NZ)
            orders.append(jnp.where(eye, meta[zs * NY + y, 0:1, :].astype(jnp.float32), 0.0))
        order = jnp.sum(jnp.concatenate(orders, axis=0), axis=1, keepdims=True).astype(jnp.int32)
        lanes = lax.broadcasted_iota(jnp.int32, (count * rows, 128), 1)
        ahead = order - lanes * rows
        inside = (ahead >= 0) & (ahead < rows)
        picked = jnp.where(inside, 1.0, 0.0).astype(jnp.bfloat16)
        ids = 256.0 * jnp.dot(picked, high_ids, preferred_element_type=jnp.float32) + jnp.dot(
            picked, low_ids, preferred_element_type=jnp.float32
        )
        place_in = jnp.sum(jnp.where(inside, ahead.astype(jnp.float32), 0.0), axis=1, keepdims=True)
        wanted = jnp.sum(jnp.where(lanes == place_in.astype(jnp.int32), ids, 0.0), axis=1, keepdims=True)
        gap = wanted.astype(jnp.int32) - lanes
        founds = []
        for i, s in enumerate(slots):
            own_gap = gap[i * rows:(i + 1) * rows, :]
            found = jnp.zeros((rows, 128), jnp.float32)
            for r in range(4):
                base = (z * NY + lax.rem(y + OFFSETS[r], NY)) * cols
                for c in range(0, cols, 128):
                    found += jnp.where(own_gap == base + c, lg[r, s * rows:(s + 1) * rows, c:c + 128], 0.0)
            founds.append(found)
        target = jnp.sum(jnp.concatenate(founds, axis=0), axis=1, keepdims=True)
        lane_peak = mx[here, :]
        peak = jnp.max(lane_peak, axis=1, keepdims=True)
        fade = jnp.exp(lane_peak - peak)
        total = jnp.sum(sm[here, :] * fade, axis=1, keepdims=True)
        weighted = jnp.sum(wt[here, :] * fade, axis=1, keepdims=True)
        for i, s in enumerate(slots):
            place = stg if s == 0 else st
            for row, column in enumerate((peak, total, weighted, target)):
                place[s, row:row + 1, :] = to_row(column[i * rows:(i + 1) * rows, :])
        for s in reversed(slots):
            if s:
                send_stats(s)

    finish_all(0, far // rows)
    ring_rows(8)
    job(far, NZ * rows - far, 0, 4)
    finish_all(far // rows, NZ - far // rows)

    for copy in stats:
        copy.wait_recv()
    peak = stg[0, 0:1, :]
    for s in range(1, NZ):
        peak = jnp.maximum(peak, stg[s, 0:1, :])
    row_total = jnp.zeros((1, 128), jnp.float32)
    row_weighted, target_logit = row_total, row_total
    for s in range(NZ):
        fade = jnp.exp(stg[s, 0:1, :] - peak)
        row_total += stg[s, 1:2, :] * fade
        row_weighted += stg[s, 2:3, :] * fade
        target_logit += stg[s, 3:4, :]
    row_total = jnp.where(lane[0:1, :] < rows, row_total, 1.0)
    lse = peak + jnp.log(row_total)
    fing[0:1, :] = target_logit - lse
    fing[1:2, :] = lse - row_weighted / row_total
    fin[tt] = fing[...]

    def final_copy(i):
        other = lax.rem(tt + i, NT)
        return pltpu.make_async_remote_copy(
            src_ref=fing, dst_ref=fin.at[tt], send_sem=c_s.at[i], recv_sem=c_r.at[i],
            device_id=(dp, other), device_id_type=MESH,
        )

    def start_final(i, carry):
        final_copy(i).start()
        return carry

    lax.fori_loop(1, NT, start_final, 0)
    sub8 = lax.broadcasted_iota(jnp.int32, (seqs, 128), 0)
    lane8 = lax.broadcasted_iota(jnp.int32, (seqs, 128), 1)
    first = jnp.zeros((seqs, 128), jnp.int32)
    last = first
    running = jnp.int32(0)
    for i in range(seqs):
        first = jnp.where(sub8 == i, running, first)
        running = running + lengths[i]
        last = jnp.where(sub8 == i, running, last)
    for copy in sent:
        copy.wait_send()

    def end_final(i, carry):
        final_copy(i).wait()
        return carry

    lax.fori_loop(1, NT, end_final, 0)
    position = tt * rows + lax.broadcasted_iota(jnp.int32, (rows, 128), 0)

    def place_rows(t, carry):
        logprob, entropy, seq_logprob, seq_entropy = carry
        order = meta[t, 0:1, :]
        got_logprob, got_entropy = fin[t, 0:1, :], fin[t, 1:2, :]
        match = order == position
        member = (order >= first) & (order < last)
        return (
            logprob + jnp.where(match, got_logprob, 0.0),
            entropy + jnp.where(match, got_entropy, 0.0),
            seq_logprob + jnp.where(member, got_logprob, 0.0),
            seq_entropy + jnp.where(member, got_entropy, 0.0),
        )

    wide, narrow = jnp.zeros((rows, 128), jnp.float32), jnp.zeros((seqs, 128), jnp.float32)
    logprob, entropy, seq_logprob, seq_entropy = lax.fori_loop(0, NT, place_rows, (wide, wide, narrow, narrow))
    out[0:1, :] = to_row(jnp.sum(logprob, axis=1, keepdims=True))
    out[1:2, :] = to_row(jnp.sum(entropy, axis=1, keepdims=True))
    counts = (last - first).astype(jnp.float32)
    for i, value in ((2, seq_logprob), (3, seq_entropy)):
        mean = jnp.sum(value, axis=1, keepdims=True) / counts
        out[i:i + 1, :] = jnp.sum(jnp.where(sub8 == lane8, mean, 0.0), axis=0, keepdims=True)


def per_device(hidden, norm_gain, head_weight, token_order, targets, lengths):
    rows, width = hidden.shape
    depth, cols = head_weight.shape
    seqs = lengths.shape[0]
    total = NZ * rows
    vmem, dma = pltpu.VMEM, pltpu.SemaphoreType.DMA
    half = NZ // 2
    out = pl.pallas_call(
        kernel,
        out_shape=jax.ShapeDtypeStruct((4, 128), jnp.float32),
        in_specs=[pl.BlockSpec(memory_space=pl.ANY)] * 6,
        out_specs=pl.BlockSpec(memory_space=pltpu.VMEM),
        scratch_shapes=[
            vmem(hidden.shape, hidden.dtype),
            vmem(norm_gain.shape, norm_gain.dtype),
            vmem((rows,), jnp.int32),
            vmem((rows,), jnp.int32),
            pltpu.SMEM((seqs,), jnp.int32),
            dma((5,)),
            vmem((total, width), jnp.bfloat16),
            vmem((4, depth, cols), jnp.bfloat16),
            vmem((4, total, cols), jnp.float32),
            vmem((NT, 2, 128), jnp.int32),
            vmem((128, 128), jnp.float32),
            vmem((128, 128), jnp.float32),
            vmem((total, 128), jnp.float32),
            vmem((total, 128), jnp.float32),
            vmem((total, 128), jnp.float32),
            vmem((NZ, 4, 128), jnp.float32),
            vmem((NZ, 4, 128), jnp.float32),
            vmem((2, 128), jnp.float32),
            vmem((NT, 2, 128), jnp.float32),
            dma,
            dma((2, half, rows // PIECE)), dma((2, half, rows // PIECE)),
            dma((2, half)), dma((2, half)),
            dma((3,)), dma((3,)),
            dma((3, 2)), dma((3, 2)),
            dma((3, 2)), dma((3, 2)),
            dma((2, 3, 2)), dma((2, 3, 2)),
            dma((NZ,)), dma((NZ,)),
            dma((NT,)), dma((NT,)),
        ],
        compiler_params=pltpu.CompilerParams(
            collective_id=0, has_side_effects=True, vmem_limit_bytes=60 * 1024 * 1024
        ),
    )(hidden, norm_gain, head_weight, token_order, targets, lengths)
    return out[0, :rows], out[1, :rows], out[2, :seqs], out[3, :seqs]


def solution(mesh):
    return jax.shard_map(
        per_device,
        mesh=mesh,
        in_specs=(
            P(("dp", "tensor"), None),
            P(),
            P(None, "tensor"),
            P(("dp", "tensor")),
            P(("dp", "tensor")),
            P("dp"),
        ),
        out_specs=(P(("dp", "tensor")), P(("dp", "tensor")), P("dp"), P("dp")),
        check_vma=False,
    )
```

```python
import functools

import jax
import jax.numpy as jnp
from jax import lax
from jax.experimental import pallas as pl
from jax.experimental.pallas import tpu as pltpu
from jax.sharding import PartitionSpec as P

MESH = pl.DeviceIdType.MESH
NX, NY, NZ = 4, 4, 16
NT = NZ * NY
PIECE = 16
SIDES = 1
OFFSETS = (NY - 1, 1, 2, 0)


def kernel(
    hid_in, gain_in, w_hbm, order_in, target_in, lengths_in, out,
    hid, gain, order_own, target_own, lengths, in_sem, xs, wb, lg, meta, thi, tlo, mx, sm, wt, st, stg, fing, fin,
    own_sem, tok_s, tok_r, met_s, met_r, my_s, my_r, wy_s, wy_r, wx_s, wx_r, wp_s, wp_r, b_s, b_r, c_s, c_r,
):
    rows, width = hid_in.shape
    depth, cols = w_hbm.shape
    seqs = lengths_in.shape[0]
    dp, tt = lax.axis_index("dp"), lax.axis_index("tensor")
    core, x = lax.rem(dp, 2), lax.div(dp, 2)
    y, z = lax.rem(tt, NY), lax.div(tt, NY)
    q = lax.rem(x, 2)

    def dev(dx=0, dy=0, dz=0, other=False):
        c = 1 - core if other else core
        return (
            lax.rem(x + dx + NX, NX) * 2 + c,
            lax.rem(z + dz + NZ, NZ) * NY + lax.rem(y + dy + NY, NY),
        )

    def send(src, dst, ssem, rsem, device):
        copy = pltpu.make_async_remote_copy(
            src_ref=src, dst_ref=dst, send_sem=ssem, recv_sem=rsem, device_id=device, device_id_type=MESH
        )
        copy.start()
        sent.append(copy)
        return copy

    sent = []
    barrier = pltpu.get_barrier_semaphore()
    friends = [dev(dy=1), dev(dy=-1), dev(dy=2), dev(dz=1), dev(dz=-1), dev(dx=1), dev(dx=-1), dev(other=True)]
    for friend in friends:
        pl.semaphore_signal(barrier, inc=1, device_id=friend, device_id_type=MESH)
    own_copy = pltpu.make_async_copy(w_hbm, wb.at[3], own_sem)
    inputs = [
        pltpu.make_async_copy(source, target, in_sem.at[i])
        for i, (source, target) in enumerate((
            (hid_in, hid), (gain_in, gain), (order_in, order_own), (target_in, target_own), (lengths_in, lengths),
        ))
    ]
    for copy in inputs:
        copy.start()
    own_copy.start()
    for copy in inputs:
        copy.wait()
    meta[tt, 0:1, :] = jnp.full((1, 128), -1, jnp.int32)
    meta[tt, 1:2, :] = jnp.zeros((1, 128), jnp.int32)
    meta[tt, 0:1, 0:rows] = order_own[...].reshape(1, rows)
    meta[tt, 1:2, 0:rows] = target_own[...].reshape(1, rows)
    values = hid[...].astype(jnp.float32)
    scale = lax.rsqrt(jnp.mean(values * values, axis=-1, keepdims=True) + 1e-05)
    xs[0:rows, :] = (values * scale * gain[...].astype(jnp.float32).reshape(1, width)).astype(jnp.bfloat16)
    mx[...] = jnp.full(mx.shape, -jnp.inf, jnp.float32)
    sm[...] = jnp.zeros_like(sm)
    wt[...] = jnp.zeros_like(wt)
    thi[...] = jnp.zeros_like(thi)
    tlo[...] = jnp.zeros_like(tlo)
    pl.semaphore_wait(barrier, len(friends))

    def slot(s, piece):
        band, side = piece // SIDES, piece % SIDES
        return xs.at[pl.ds(s * rows + band * PIECE, PIECE), pl.ds(side * (width // SIDES), width // SIDES)]

    def ways(k, piece):
        return (0, 1) if k < NZ // 2 else (piece % 2,)

    def send_tokens(k, piece, way):
        if way not in ways(k, piece):
            return
        source = (2 * k - 2 if way else max(2 * k - 3, 0))
        target = 2 * k if way and k < NZ // 2 else 2 * k - 1
        where = way, k - 1, piece
        tokens[where] = send(
            slot(source, piece), slot(target, piece), tok_s.at[where], tok_r.at[where], dev(dz=-1 if way else 1)
        )

    def send_meta(k):
        there = meta.at[pl.ds(lax.rem(z - (k - 1) + NZ, NZ) * NY, NY)]
        right = send(there, there, met_s.at[0, k - 1], met_r.at[0, k - 1], dev(dz=1))
        left = None
        if k < NZ // 2:
            there = meta.at[pl.ds(lax.rem(z + (k - 1), NZ) * NY, NY)]
            left = send(there, there, met_s.at[1, k - 1], met_r.at[1, k - 1], dev(dz=-1))
        return right, left

    def row_at(c, parity, e):
        quarter = depth // 4
        return pl.multiple_of(c * (depth // 2) + parity * quarter + e * (quarter // 2), 64)

    def part(r, c, parity, e):
        return wb.at[r, pl.ds(row_at(c, parity, e), depth // 8), :]

    def mine(e):
        return w_hbm.at[pl.ds(row_at(core, q, e), depth // 8), :]

    wy, wx, wp = {}, {}, {}

    def send_y(r, e, src, dy):
        wy[r, e] = send(src, part(r, core, q, e), wy_s.at[r, e], wy_r.at[r, e], dev(dy=dy))

    def got_y(r, e):
        wy[r, e].wait_recv()
        here = part(r, core, q, e)
        if (r, e) == (0, 0):
            send_y(2, 0, here, 1)
        if (r, e) == (1, 1):
            send_y(2, 1, here, -1)
        wx[r, e] = send(here, here, wx_s.at[r, e], wx_r.at[r, e], dev(dx=1 if e == 0 else -1))
        wp[0, r, e] = send(here, here, wp_s.at[0, r, e], wp_r.at[0, r, e], dev(other=True))

    def got_x(r, e):
        wx[r, e].wait_recv()
        here = part(r, core, 1 - q, e)
        wp[1, r, e] = send(here, here, wp_s.at[1, r, e], wp_r.at[1, r, e], dev(other=True))

    def got_partner(r):
        for source in (0, 1):
            for e in (0, 1):
                wp[source, r, e].wait_recv()

    def job(first, count, r_first, r_count):
        here = pl.ds(first, count)

        def step(i, carry):
            r = lax.rem(r_first + i, 4)
            logits = jnp.dot(xs[here, :], wb[r], preferred_element_type=jnp.float32)
            parts = [logits[:, c:c + 128] for c in range(0, cols, 128)]
            lg[r, here, :] = logits
            old = mx[here, :]
            peak = functools.reduce(jnp.maximum, parts, old)
            fade = jnp.exp(old - peak)
            total, weighted = sm[here, :] * fade, wt[here, :] * fade
            for piece in parts:
                exponent = jnp.exp(piece - peak)
                total += exponent
                weighted += exponent * piece
            mx[here, :], sm[here, :], wt[here, :] = peak, total, weighted
            return carry

        lax.fori_loop(0, r_count, step, 0)

    pieces = rows // PIECE * SIDES
    tokens = {}
    for piece in range(pieces):
        for way in (0, 1):
            send_tokens(1, piece, way)
    metas = {}
    meta_y = [
        send(meta.at[tt], meta.at[tt], my_s.at[i], my_r.at[i], dev(dy=dy)) for i, dy in enumerate((1, -1, 2))
    ]
    send_y(0, 0, mine(0), 1)
    send_y(1, 1, mine(1), -1)
    send_y(0, 1, mine(1), 1)
    send_y(1, 0, mine(0), -1)
    for copy in meta_y:
        copy.wait_recv()
    metas[1] = send_meta(1)

    def ring_meta(k):
        for copy in metas[k]:
            if copy is not None:
                copy.wait_recv()
        if k < NZ // 2:
            metas[k + 1] = send_meta(k + 1)

    def ring_rows(k):
        for piece in range(pieces):
            for way in ways(k, piece):
                tokens[way, k - 1, piece].wait_recv()
                if k < NZ // 2:
                    send_tokens(k + 1, piece, way)

    def ring(k):
        ring_meta(k)
        ring_rows(k)

    near, mid, far = 5 * rows, 9 * rows, 13 * rows
    ring(1)
    got_y(0, 0)
    got_y(1, 1)
    ring(2)
    own_copy.wait()
    job(0, near, 3, 1)
    ring(3)
    got_y(0, 1)
    got_y(1, 0)
    got_x(0, 0)
    got_x(1, 1)
    ring(4)
    got_y(2, 0)
    got_y(2, 1)
    got_x(0, 1)
    got_x(1, 0)
    job(near, mid - near, 3, 1)
    ring(5)
    got_partner(0)
    got_partner(1)
    job(0, mid, 0, 1)
    ring(6)
    got_x(2, 0)
    got_x(2, 1)
    job(0, mid, 1, 1)
    job(mid, far - mid, 3, 3)
    ring(7)
    got_partner(2)
    job(0, far, 2, 1)
    ring_meta(8)

    lane = lax.broadcasted_iota(jnp.int32, (rows, 128), 1)
    eye = lane == lax.broadcasted_iota(jnp.int32, (rows, 128), 0)
    for t in range(NT):
        ids = meta[t, 1:2, :]
        high = ids >> 8
        thi[t:t + 1, :] = high.astype(jnp.float32)
        tlo[t:t + 1, :] = (ids - (high << 8)).astype(jnp.float32)
    high_ids, low_ids = thi[...].astype(jnp.bfloat16), tlo[...].astype(jnp.bfloat16)

    def to_row(column):
        return jnp.sum(jnp.where(eye, column, 0.0), axis=0, keepdims=True)

    stats = []

    def send_stats(s):
        k = (s + 1) // 2
        if s % 2:
            theirs, dz = (2 * k if k < NZ // 2 else s), -k
        else:
            theirs, dz = 2 * k - 1, k
        stats.append(send(st.at[s], stg.at[theirs], b_s.at[s], b_r.at[theirs], dev(dz=dz)))

    def finish_all(first, count):
        slots, here = range(first, first + count), pl.ds(first * rows, count * rows)
        orders = []
        for s in slots:
            k = (s + 1) // 2
            zs = lax.rem(z + (-k if s % 2 else k) + NZ, NZ)
            orders.append(jnp.where(eye, meta[zs * NY + y, 0:1, :].astype(jnp.float32), 0.0))
        order = jnp.sum(jnp.concatenate(orders, axis=0), axis=1, keepdims=True).astype(jnp.int32)
        lanes = lax.broadcasted_iota(jnp.int32, (count * rows, 128), 1)
        ahead = order - lanes * rows
        inside = (ahead >= 0) & (ahead < rows)
        picked = jnp.where(inside, 1.0, 0.0).astype(jnp.bfloat16)
        ids = 256.0 * jnp.dot(picked, high_ids, preferred_element_type=jnp.float32) + jnp.dot(
            picked, low_ids, preferred_element_type=jnp.float32
        )
        place_in = jnp.sum(jnp.where(inside, ahead.astype(jnp.float32), 0.0), axis=1, keepdims=True)
        wanted = jnp.sum(jnp.where(lanes == place_in.astype(jnp.int32), ids, 0.0), axis=1, keepdims=True)
        gap = wanted.astype(jnp.int32) - lanes
        founds = []
        for i, s in enumerate(slots):
            own_gap = gap[i * rows:(i + 1) * rows, :]
            found = jnp.zeros((rows, 128), jnp.float32)
            for r in range(4):
                base = (z * NY + lax.rem(y + OFFSETS[r], NY)) * cols
                for c in range(0, cols, 128):
                    found += jnp.where(own_gap == base + c, lg[r, s * rows:(s + 1) * rows, c:c + 128], 0.0)
            founds.append(found)
        target = jnp.sum(jnp.concatenate(founds, axis=0), axis=1, keepdims=True)
        lane_peak = mx[here, :]
        peak = jnp.max(lane_peak, axis=1, keepdims=True)
        fade = jnp.exp(lane_peak - peak)
        total = jnp.sum(sm[here, :] * fade, axis=1, keepdims=True)
        weighted = jnp.sum(wt[here, :] * fade, axis=1, keepdims=True)
        for i, s in enumerate(slots):
            place = stg if s == 0 else st
            for row, column in enumerate((peak, total, weighted, target)):
                place[s, row:row + 1, :] = to_row(column[i * rows:(i + 1) * rows, :])
        for s in reversed(slots):
            if s:
                send_stats(s)

    finish_all(0, far // rows)
    ring_rows(8)
    job(far, NZ * rows - far, 0, 4)
    finish_all(far // rows, NZ - far // rows)

    for copy in stats:
        copy.wait_recv()
    peak = stg[0, 0:1, :]
    for s in range(1, NZ):
        peak = jnp.maximum(peak, stg[s, 0:1, :])
    row_total = jnp.zeros((1, 128), jnp.float32)
    row_weighted, target_logit = row_total, row_total
    for s in range(NZ):
        fade = jnp.exp(stg[s, 0:1, :] - peak)
        row_total += stg[s, 1:2, :] * fade
        row_weighted += stg[s, 2:3, :] * fade
        target_logit += stg[s, 3:4, :]
    row_total = jnp.where(lane[0:1, :] < rows, row_total, 1.0)
    lse = peak + jnp.log(row_total)
    fing[0:1, :] = target_logit - lse
    fing[1:2, :] = lse - row_weighted / row_total
    fin[tt] = fing[...]

    def final_copy(i):
        other = lax.rem(tt + i, NT)
        return pltpu.make_async_remote_copy(
            src_ref=fing, dst_ref=fin.at[tt], send_sem=c_s.at[i], recv_sem=c_r.at[i],
            device_id=(dp, other), device_id_type=MESH,
        )

    def start_final(j, carry):
        final_copy(1 + lax.rem(j + 24, NT - 1)).start()
        return carry

    lax.fori_loop(0, NT - 1, start_final, 0)
    sub8 = lax.broadcasted_iota(jnp.int32, (seqs, 128), 0)
    lane8 = lax.broadcasted_iota(jnp.int32, (seqs, 128), 1)
    first = jnp.zeros((seqs, 128), jnp.int32)
    last = first
    running = jnp.int32(0)
    for i in range(seqs):
        first = jnp.where(sub8 == i, running, first)
        running = running + lengths[i]
        last = jnp.where(sub8 == i, running, last)
    for copy in sent:
        copy.wait_send()

    def end_final(i, carry):
        final_copy(i).wait()
        return carry

    lax.fori_loop(1, NT, end_final, 0)
    position = tt * rows + lax.broadcasted_iota(jnp.int32, (rows, 128), 0)

    def place_rows(t, carry):
        logprob, entropy, seq_logprob, seq_entropy = carry
        order = meta[t, 0:1, :]
        got_logprob, got_entropy = fin[t, 0:1, :], fin[t, 1:2, :]
        match = order == position
        member = (order >= first) & (order < last)
        return (
            logprob + jnp.where(match, got_logprob, 0.0),
            entropy + jnp.where(match, got_entropy, 0.0),
            seq_logprob + jnp.where(member, got_logprob, 0.0),
            seq_entropy + jnp.where(member, got_entropy, 0.0),
        )

    wide, narrow = jnp.zeros((rows, 128), jnp.float32), jnp.zeros((seqs, 128), jnp.float32)
    logprob, entropy, seq_logprob, seq_entropy = lax.fori_loop(
        0, NT, place_rows, (wide, wide, narrow, narrow), unroll=4
    )
    out[0:1, :] = to_row(jnp.sum(logprob, axis=1, keepdims=True))
    out[1:2, :] = to_row(jnp.sum(entropy, axis=1, keepdims=True))
    counts = (last - first).astype(jnp.float32)
    for i, value in ((2, seq_logprob), (3, seq_entropy)):
        mean = jnp.sum(value, axis=1, keepdims=True) / counts
        out[i:i + 1, :] = jnp.sum(jnp.where(sub8 == lane8, mean, 0.0), axis=0, keepdims=True)


def per_device(hidden, norm_gain, head_weight, token_order, targets, lengths):
    rows, width = hidden.shape
    depth, cols = head_weight.shape
    seqs = lengths.shape[0]
    total = NZ * rows
    vmem, dma = pltpu.VMEM, pltpu.SemaphoreType.DMA
    half = NZ // 2
    out = pl.pallas_call(
        kernel,
        out_shape=jax.ShapeDtypeStruct((4, 128), jnp.float32),
        in_specs=[pl.BlockSpec(memory_space=pl.ANY)] * 6,
        out_specs=pl.BlockSpec(memory_space=pltpu.VMEM),
        scratch_shapes=[
            vmem(hidden.shape, hidden.dtype),
            vmem(norm_gain.shape, norm_gain.dtype),
            vmem((rows,), jnp.int32),
            vmem((rows,), jnp.int32),
            pltpu.SMEM((seqs,), jnp.int32),
            dma((5,)),
            vmem((total, width), jnp.bfloat16),
            vmem((4, depth, cols), jnp.bfloat16),
            vmem((4, total, cols), jnp.float32),
            vmem((NT, 2, 128), jnp.int32),
            vmem((128, 128), jnp.float32),
            vmem((128, 128), jnp.float32),
            vmem((total, 128), jnp.float32),
            vmem((total, 128), jnp.float32),
            vmem((total, 128), jnp.float32),
            vmem((NZ, 4, 128), jnp.float32),
            vmem((NZ, 4, 128), jnp.float32),
            vmem((2, 128), jnp.float32),
            vmem((NT, 2, 128), jnp.float32),
            dma,
            dma((2, half, rows // PIECE * SIDES)), dma((2, half, rows // PIECE * SIDES)),
            dma((2, half)), dma((2, half)),
            dma((3,)), dma((3,)),
            dma((3, 2)), dma((3, 2)),
            dma((3, 2)), dma((3, 2)),
            dma((2, 3, 2)), dma((2, 3, 2)),
            dma((NZ,)), dma((NZ,)),
            dma((NT,)), dma((NT,)),
        ],
        compiler_params=pltpu.CompilerParams(
            collective_id=0, has_side_effects=True, vmem_limit_bytes=60 * 1024 * 1024
        ),
    )(hidden, norm_gain, head_weight, token_order, targets, lengths)
    return out[0, :rows], out[1, :rows], out[2, :seqs], out[3, :seqs]


def solution(mesh):
    return jax.shard_map(
        per_device,
        mesh=mesh,
        in_specs=(
            P(("dp", "tensor"), None),
            P(),
            P(None, "tensor"),
            P(("dp", "tensor")),
            P(("dp", "tensor")),
            P("dp"),
        ),
        out_specs=(P(("dp", "tensor")), P(("dp", "tensor")), P("dp"), P("dp")),
        check_vma=False,
    )
```
